256 devices in a mesh: pencil: 64 (over z, y_lo, x), lev: 4 (over y_hi, core).
Axes of the slice: x: 4, y: 4 (y_hi: 2, y_lo: 2; y = y_hi * 2 + y_lo), z: 8, core: 2. Of those that a mesh axis runs over, the one named last changes fastest.
Arguments:
- increment: bfloat16 [4, 4, 4096, 2048], P(None, 'lev', 'pencil'), may hold values from -6 to 6
- vert_coef: float32 [4, 4, 3], replicated, may hold values from -3 to 3
- latitude_block_matrix: bfloat16 [8, 5, 128, 128], replicated, may hold values from -0.25 to 0.25
- lat_band: int32 [16], replicated, may hold values from 0 to 7
- lat_offsets: int32 [5], replicated, may hold values from -3 to 3, as said below
- lon_blocks: bfloat16 [5, 128, 128], replicated, may hold values from -0.25 to 0.25
- lon_offsets: int32 [5], replicated, may hold values from -3 to 3, as said below
Outputs:
- filtered: float32 [2048, 4, 4, 4096], P('pencil', None, 'lev')
The draws below stay inside these ranges and needn't reach their ends.
Inputs may be any that keep to these rules, and one draw needn't show every extreme that they name: `lat_offsets`: 5 distinct offsets, -3 and 3 always among them. `lon_offsets`: 5 distinct offsets, -3 and 3 always among them.
All inputs are finite; a program needn't handle non-finite values.
Results may differ from the reference program's by a relative error of at most 0.0041.
Values may be sent and summed in bfloat16 or wider, within the bound.
No kernel may reach another device: no remote copies, remote signals or barrier semaphores. Data moves between devices by JAX's collectives and lax.ppermute only.
A program may use at most 64 MiB of HBM per device.

```python
import jax
import jax.numpy as jnp
from jax import lax

NLON = 4096
NLAT = 2048
NV = 4
BLK = 128
TAPS = 5
NBANDS = 8
LEV = 4
NBLAT = 16


def offsets_from(key):
    middle = jax.random.permutation(key, jnp.arange(-2, 3, dtype=jnp.int32))[:TAPS - 2]
    full = jnp.concatenate([jnp.array([-3, 3], dtype=jnp.int32), middle])
    return jax.random.permutation(jax.random.fold_in(key, 1), full)


def draw_lat_offsets(key, part):
    return offsets_from(jax.random.fold_in(key, 11))


def draw_lon_offsets(key, part):
    return offsets_from(jax.random.fold_in(key, 23))


def place_ends(values, stream_key, low, top_value):
    longest = values.shape.index(max(values.shape))
    spots = []
    for shift in (0, 1):
        where = [jax.random.randint(jax.random.fold_in(stream_key, axis), (), 0, length) for axis, length in enumerate(values.shape)]
        where[longest] = (where[longest] + shift) % values.shape[longest]
        spots.append(tuple(where))
    return values.at[spots[0]].set(low).at[spots[1]].set(top_value)


def block_scale(stream_key, dims, shards, least, high):
    level = 1.0
    for position, shards_of in shards:
        heights = jax.random.uniform(jax.random.fold_in(jax.random.fold_in(stream_key, 6), position), (shards_of,), jnp.float32, least / len(shards), high / len(shards))
        level = level * jnp.repeat(jnp.exp(heights), dims[position] // shards_of).reshape((-1,) + (1,) * (len(dims) - 1 - position))
    return level


def gaussian(key, dims, spread, bound, cuts=(), held_as=jnp.bfloat16):
    gain = block_scale(key, dims, cuts, -0.22, 0.18) if cuts else 1.0
    values = jax.random.normal(key, dims, jnp.float32) * spread * gain
    return jnp.minimum(jnp.maximum(values, -bound), bound).astype(held_as)


def setup_inputs(seed: int = 0) -> dict:
    seeds = jax.random.split(jax.random.key(seed), 8)
    return {
        "increment": gaussian(seeds[0], (NV, LEV, NLON, NLAT), 1.0, 6.0, ((1, 4), (2, 64))),
        "vert_coef": gaussian(seeds[1], (NV, LEV, 3), 0.5, 3.0, (), jnp.float32),
        "latitude_block_matrix": gaussian(seeds[2], (NBANDS, TAPS, BLK, BLK), (TAPS * BLK) ** -0.5, 0.25),
        "lat_band": place_ends(jax.random.randint(seeds[3], (NBLAT,), 0, NBANDS), jax.random.fold_in(seeds[3], 1), 0, NBANDS - 1).astype(jnp.int32),
        "lat_offsets": draw_lat_offsets(jax.random.fold_in(seeds[7], 71), 0),
        "lon_blocks": gaussian(seeds[5], (TAPS, BLK, BLK), (TAPS * BLK) ** -0.5, 0.25),
        "lon_offsets": draw_lon_offsets(jax.random.fold_in(seeds[7], 71), 0),
    }


def latitude_weight_rows(latitude_block_matrix, lat_band, lat_offsets):
    count = lat_band.shape[0]
    block_ids = jnp.arange(count, dtype=jnp.int32)[:, None] - lat_offsets[None, :]
    clipped = jnp.clip(block_ids, 0, count - 1)
    shifted = lat_band[clipped]
    selector_matrix = (shifted[:, :, None] == jnp.arange(latitude_block_matrix.shape[0], dtype=jnp.int32)[None, None, :]).astype(jnp.float32)
    table = jnp.einsum("skb,bkij->skij", selector_matrix, latitude_block_matrix.astype(jnp.float32))
    return table.reshape(count, -1, latitude_block_matrix.shape[-1])


def lat_apply(flat_rows, weight_matrix, offsets):
    size = weight_matrix.shape[-1]
    rows, nlat = flat_rows.shape
    nblk = nlat // size
    padded = jnp.pad(flat_rows, ((0, 0), (3 * size, 3 * size)))
    pieces = [lax.dynamic_slice_in_dim(padded, (3 - offsets[k]) * size, nlat, axis=1).reshape(rows, nblk, size) for k in range(offsets.shape[0])]
    collected_rows = jnp.concatenate(pieces, axis=-1)
    adjoint_output = jnp.einsum("eod,odv->ove", collected_rows, weight_matrix)
    return adjoint_output.reshape(nlat, rows)


def lon_apply(block_in, blocks, offsets):
    size = blocks.shape[-1]
    width = block_in.shape[-1]
    nblk = width // size
    rolled = [jnp.roll(block_in, offsets[k] * size, axis=-1).reshape(block_in.shape[:-1] + (nblk, size)) for k in range(blocks.shape[0])]
    stacked = jnp.concatenate(rolled, axis=-1)
    adjoint_output = jnp.einsum("...sq,qc->...sc", stacked, blocks.reshape(-1, size))
    return adjoint_output.reshape(block_in.shape)


def reference(increment, vert_coef, latitude_block_matrix, lat_band, lat_offsets, lon_blocks, lon_offsets):
    weight_matrix = latitude_weight_rows(latitude_block_matrix, lat_band, lat_offsets).astype(jnp.bfloat16).astype(jnp.float32)
    lon_float = lon_blocks.astype(jnp.float32)
    padded_coef = jnp.pad(vert_coef, ((0, 0), (1, 1), (0, 0)))
    nlon = increment.shape[2]
    nlat = increment.shape[3]

    def one_plane(flat_index):
        var_index = flat_index // LEV
        level = flat_index % LEV
        total = jnp.zeros((nlon, nlat), jnp.float32)
        for m in range(3):
            source = jnp.clip(level - 1 + m, 0, LEV - 1).astype(jnp.int32)
            slab = lax.dynamic_slice(increment, (var_index, source, jnp.int32(0), jnp.int32(0)), (1, 1, nlon, nlat))[0, 0]
            weight = padded_coef[var_index, level + m, 2 - m]
            total = total + weight * slab.astype(jnp.float32)
        vertical = total.astype(jnp.bfloat16).astype(jnp.float32)
        lat_filtered = lat_apply(vertical, weight_matrix, lat_offsets).astype(jnp.bfloat16).astype(jnp.float32)
        return lon_apply(lat_filtered, lon_float, lon_offsets)

    planes = lax.map(one_plane, jnp.arange(NV * LEV, dtype=jnp.int32))
    planes = planes.reshape(NV, LEV, nlat, nlon)
    return jnp.transpose(planes, (2, 0, 1, 3))
```

```python
import jax
import jax.numpy as jnp
from jax import lax
from jax.experimental import pallas as pl
from jax.experimental.pallas import tpu as pltpu
from jax.sharding import PartitionSpec as P

BLK = 128
REACH = 3


def lat_kernel(nblk, coef, band, offs, lev, own, below, above, table, out, blocks):
    variables, _, rows, _ = own.shape
    levels = coef.shape[1]
    taps = offs.shape[0]
    level = lev[0]
    lower = jnp.maximum(level - 1, 0)
    upper = jnp.minimum(level + 1, levels - 1)
    zeros = jnp.zeros(blocks.shape[1:], blocks.dtype)
    for edge in range(REACH):
        blocks[edge] = zeros
        blocks[REACH + nblk + edge] = zeros
    for v in range(variables):
        c_below = jnp.where(level > 0, coef[v, lower, 2], 0.0)
        c_own = coef[v, level, 1]
        c_above = jnp.where(level < levels - 1, coef[v, upper, 0], 0.0)
        for t in range(nblk):
            cols = slice(t * BLK, (t + 1) * BLK)
            total = c_below * below[v, 0, :, cols].astype(jnp.float32)
            total = total + c_own * own[v, 0, :, cols].astype(jnp.float32)
            total = total + c_above * above[v, 0, :, cols].astype(jnp.float32)
            blocks[REACH + t, v * rows : (v + 1) * rows, :] = total.astype(blocks.dtype)
    for s in range(nblk):
        lhs, rhs = [], []
        for k in range(taps):
            source = s - offs[k]
            lhs.append(blocks[source + REACH])
            rhs.append(table[band[jnp.clip(source, 0, nblk - 1)], k])
        total = jnp.dot(
            jnp.concatenate(lhs, axis=1),
            jnp.concatenate(rhs, axis=0),
            preferred_element_type=jnp.float32,
        )
        out[s * BLK : (s + 1) * BLK, :] = total.T.astype(out.dtype)


def lon_kernel(offs, data, weights, out, blocks):
    peers, lats, width = data.shape
    variables = width // (BLK // 2)
    nblk = peers // 2
    taps = offs.shape[0]
    group = 8
    half = BLK // 2
    first = lax.broadcasted_iota(jnp.int32, (lats, BLK), 1) < half
    for t in range(nblk):
        for pair in range(variables // 2):
            cols = slice(pair * BLK, (pair + 1) * BLK)
            a = data[2 * t, :, cols].astype(jnp.float32)
            b = data[2 * t + 1, :, cols].astype(jnp.float32)
            even = jnp.where(first, a, pltpu.roll(b, half, 1))
            odd = jnp.where(first, pltpu.roll(a, half, 1), b)
            v = 2 * pair
            blocks[t, v * lats : (v + 1) * lats, :] = even.astype(blocks.dtype)
            blocks[t, (v + 1) * lats : (v + 2) * lats, :] = odd.astype(blocks.dtype)
    rhs = jnp.concatenate([weights[k] for k in range(taps)], axis=0)
    for g in range(0, nblk, group):
        lhs = []
        for s in range(g, g + group):
            lhs.append(
                jnp.concatenate(
                    [blocks[lax.rem(s - offs[k] + nblk, nblk)] for k in range(taps)], axis=1
                )
            )
        total = jnp.dot(
            jnp.concatenate(lhs, axis=0), rhs, preferred_element_type=jnp.float32
        )
        for n, s in enumerate(range(g, g + group)):
            for v in range(variables):
                row = (n * variables + v) * lats
                out[pl.ds(v * nblk + s, lats, stride=variables * nblk), :] = total[
                    row : row + lats
                ]


def per_device(
    increment, vert_coef, latitude_block_matrix, lat_band, lat_offsets, lon_blocks, lon_offsets
):
    variables, _, rows, nlat = increment.shape
    nblk = nlat // BLK
    npencil = lax.axis_size("pencil")
    nlev = lax.axis_size("lev")
    nlon = rows * npencil
    lats = nlat // npencil
    smem = pl.BlockSpec(memory_space=pltpu.SMEM)
    vmem = pl.BlockSpec(memory_space=pltpu.VMEM)

    below = lax.ppermute(increment, "lev", [(n, n + 1) for n in range(nlev - 1)])
    above = lax.ppermute(increment, "lev", [(n + 1, n) for n in range(nlev - 1)])
    own_level = lax.axis_index("lev").astype(jnp.int32).reshape(1)

    filtered = pl.pallas_call(
        lambda *refs: lat_kernel(nblk, *refs),
        out_shape=jax.ShapeDtypeStruct((nlat, variables * rows), jnp.bfloat16),
        in_specs=[smem] * 4 + [vmem] * 4,
        out_specs=vmem,
        scratch_shapes=[pltpu.VMEM((nblk + 2 * REACH, variables * rows, BLK), jnp.bfloat16)],
        compiler_params=pltpu.CompilerParams(vmem_limit_bytes=40 * 2**20),
        name="vertical_and_latitude",
    )(vert_coef, lat_band, lat_offsets, own_level, increment, below, above, latitude_block_matrix)

    moved = lax.all_to_all(filtered, "pencil", split_axis=0, concat_axis=0, tiled=True)

    result = pl.pallas_call(
        lon_kernel,
        out_shape=jax.ShapeDtypeStruct((lats * variables * nlon // BLK, BLK), jnp.float32),
        in_specs=[smem, vmem, vmem],
        out_specs=vmem,
        scratch_shapes=[pltpu.VMEM((nlon // BLK, lats * variables, BLK), jnp.bfloat16)],
        compiler_params=pltpu.CompilerParams(vmem_limit_bytes=40 * 2**20),
        name="longitude",
    )(lon_offsets, moved.reshape(npencil, lats, variables * rows), lon_blocks)
    return result.reshape(lats, variables, 1, nlon)


def solution(mesh):
    in_specs = (P(None, "lev", "pencil", None), P(), P(), P(), P(), P(), P())
    out_specs = P("pencil", None, "lev", None)
    return jax.shard_map(
        per_device, mesh=mesh, in_specs=in_specs, out_specs=out_specs, check_vma=False
    )
```

```python
import jax
import jax.numpy as jnp
from jax import lax
from jax.experimental import pallas as pl
from jax.experimental.pallas import tpu as pltpu
from jax.sharding import PartitionSpec as P

BLK = 128
REACH = 3
CHUNKS = 1


def weight_kernel(band, offs, table, out):
    nblk = band.shape[0]
    taps = offs.shape[0]
    for s in range(nblk):
        for k in range(taps):
            source = jnp.clip(s - offs[k], 0, nblk - 1)
            out[s, k * BLK : (k + 1) * BLK, :] = table[band[source], k]


def lat_kernel(chunk, coef, offs, lev, own, below, above, weights, out, blocks):
    variables, _, rows, nlat = own.shape
    nblk = nlat // BLK
    levels = coef.shape[1]
    taps = offs.shape[0]
    level = lev[0]
    lower = jnp.maximum(level - 1, 0)
    upper = jnp.minimum(level + 1, levels - 1)
    zeros = jnp.zeros(blocks.shape[1:], blocks.dtype)
    for edge in range(REACH):
        blocks[edge] = zeros
        blocks[REACH + nblk + edge] = zeros
    for n in range(variables):
        v = chunk * variables + n
        c_below = jnp.where(level > 0, coef[v, lower, 2], 0.0)
        c_own = coef[v, level, 1]
        c_above = jnp.where(level < levels - 1, coef[v, upper, 0], 0.0)
        for t in range(nblk):
            cols = slice(t * BLK, (t + 1) * BLK)
            total = c_below * below[n, 0, :, cols].astype(jnp.float32)
            total = total + c_own * own[n, 0, :, cols].astype(jnp.float32)
            total = total + c_above * above[n, 0, :, cols].astype(jnp.float32)
            blocks[REACH + t, n * rows : (n + 1) * rows, :] = total.astype(blocks.dtype)
    for s in range(nblk):
        lhs = [blocks[s - offs[k] + REACH] for k in range(taps)]
        total = jnp.dot(
            jnp.concatenate(lhs, axis=1), weights[s], preferred_element_type=jnp.float32
        )
        out[s * BLK : (s + 1) * BLK, :] = total.T.astype(out.dtype)


def lon_kernel(chunk, offs, data, weights, *refs):
    out, blocks, stage, sem = refs[-4:]
    peers, lats, width = data.shape
    half = BLK // 2
    variables = width // half
    nblk = peers // 2
    taps = offs.shape[0]
    group = 8
    first = lax.broadcasted_iota(jnp.int32, (lats, BLK), 1) < half
    for t in range(nblk):
        for pair in range(variables // 2):
            cols = slice(pair * BLK, (pair + 1) * BLK)
            a = data[2 * t, :, cols].astype(jnp.float32)
            b = data[2 * t + 1, :, cols].astype(jnp.float32)
            even = jnp.where(first, a, pltpu.roll(b, half, 1))
            odd = jnp.where(first, pltpu.roll(a, half, 1), b)
            v = 2 * pair
            blocks[t, v * lats : (v + 1) * lats, :] = even.astype(blocks.dtype)
            blocks[t, (v + 1) * lats : (v + 2) * lats, :] = odd.astype(blocks.dtype)
    rhs = jnp.concatenate([weights[k] for k in range(taps)], axis=0)
    rows = variables * lats
    for g in range(0, nblk, group):
        lhs = []
        for s in range(g, g + group):
            lhs.append(
                jnp.concatenate(
                    [blocks[lax.rem(s - offs[k] + nblk, nblk)] for k in range(taps)], axis=1
                )
            )
        total = jnp.dot(
            jnp.concatenate(lhs, axis=0), rhs, preferred_element_type=jnp.float32
        )
        for n, s in enumerate(range(g, g + group)):
            stage[s] = total[n * rows : (n + 1) * rows]
            for v in range(variables):
                pltpu.make_async_copy(
                    stage.at[s, v * lats : (v + 1) * lats],
                    out.at[:, chunk * variables + v, s, 0, :],
                    sem,
                ).start()
    pltpu.make_async_copy(stage, stage, sem).wait()


def per_device(
    increment, vert_coef, latitude_block_matrix, lat_band, lat_offsets, lon_blocks, lon_offsets
):
    variables, _, rows, nlat = increment.shape
    nblk = nlat // BLK
    npencil = lax.axis_size("pencil")
    nlev = lax.axis_size("lev")
    nlon = rows * npencil
    lats = nlat // npencil
    taps = lat_offsets.shape[0]
    each = variables // CHUNKS
    smem = pl.BlockSpec(memory_space=pltpu.SMEM)
    vmem = pl.BlockSpec(memory_space=pltpu.VMEM)
    hbm = pl.BlockSpec(memory_space=pl.ANY)
    up = [(n, n + 1) for n in range(nlev - 1)]
    down = [(n + 1, n) for n in range(nlev - 1)]
    own_level = lax.axis_index("lev").astype(jnp.int32).reshape(1)
    params = pltpu.CompilerParams(vmem_limit_bytes=32 * 2**20)

    parts = [increment[c * each : (c + 1) * each] for c in range(CHUNKS)]
    below = [lax.ppermute(part, "lev", up) for part in parts]
    above = [lax.ppermute(part, "lev", down) for part in parts]

    weights = pl.pallas_call(
        weight_kernel,
        out_shape=jax.ShapeDtypeStruct((nblk, taps * BLK, BLK), jnp.bfloat16),
        in_specs=[smem, smem, vmem],
        out_specs=vmem,
        compiler_params=params,
        name="latitude_weights",
    )(lat_band, lat_offsets, latitude_block_matrix)

    width = each * rows
    moved = []
    for c in range(CHUNKS):
        filtered = pl.pallas_call(
            lambda *refs, c=c: lat_kernel(c, *refs),
            out_shape=jax.ShapeDtypeStruct((nlat, width), jnp.bfloat16),
            in_specs=[smem] * 3 + [vmem] * 4,
            out_specs=vmem,
            scratch_shapes=[pltpu.VMEM((nblk + 2 * REACH, width, BLK), jnp.bfloat16)],
            compiler_params=params,
            cost_estimate=pl.CostEstimate(
                flops=2 * nlat * width * taps * BLK,
                bytes_accessed=8 * nlat * width,
                transcendentals=0,
            ),
            name=f"latitude_{c}",
        )(vert_coef, lat_offsets, own_level, parts[c], below[c], above[c], weights)
        moved.append(
            lax.all_to_all(filtered, "pencil", split_axis=0, concat_axis=0, tiled=True)
        )

    nout = nlon // BLK
    result = ()
    for c in range(CHUNKS):
        result = (
            pl.pallas_call(
                lambda *refs, c=c: lon_kernel(c, *refs),
                out_shape=jax.ShapeDtypeStruct((lats, variables, nout, 1, BLK), jnp.float32),
                in_specs=[smem, vmem, vmem] + [hbm] * len(result),
                out_specs=hbm,
                scratch_shapes=[
                    pltpu.VMEM((nout, lats * each, BLK), jnp.bfloat16),
                    pltpu.VMEM((nout, lats * each, BLK), jnp.float32),
                    pltpu.SemaphoreType.DMA,
                ],
                input_output_aliases={3: 0} if result else {},
                compiler_params=params,
                cost_estimate=pl.CostEstimate(
                    flops=2 * nlon * lats * each * taps * BLK,
                    bytes_accessed=6 * nlat * width,
                    transcendentals=0,
                ),
                name=f"longitude_{c}",
            )(lon_offsets, moved[c].reshape(npencil, lats, width), lon_blocks, *result),
        )
    return result[0].reshape(lats, variables, 1, nlon)


def solution(mesh):
    in_specs = (P(None, "lev", "pencil", None), P(), P(), P(), P(), P(), P())
    out_specs = P("pencil", None, "lev", None)
    return jax.shard_map(
        per_device, mesh=mesh, in_specs=in_specs, out_specs=out_specs, check_vma=False
    )
```

```python
import jax
import jax.numpy as jnp
from jax import lax
from jax.experimental import pallas as pl
from jax.experimental.pallas import tpu as pltpu
from jax.sharding import PartitionSpec as P

BLK = 128
REACH = 3
SPAN = 2 * REACH + 2


def operator_kernel(
    band_hbm, lat_offs_hbm, lon_offs_hbm, coef_hbm, table_hbm, lon_hbm,
    lat_out, lon_out, coef_out,
    band, lat_offs, lon_offs, coef, table, lon, sems,
):
    moves = [
        pltpu.make_async_copy(source, target, sems.at[n])
        for n, (source, target) in enumerate(
            (
                (band_hbm, band),
                (lat_offs_hbm, lat_offs),
                (lon_offs_hbm, lon_offs),
                (coef_hbm, coef),
                (table_hbm, table),
                (lon_hbm, lon),
            )
        )
    ]
    for move in moves:
        move.start()
    level = lax.axis_index("lev")
    lat_out[...] = jnp.zeros_like(lat_out)
    lon_out[...] = jnp.zeros_like(lon_out)
    for move in moves:
        move.wait()
    variables, levels, _ = coef.shape
    taps = lat_offs.shape[0]
    nblk = band.shape[0]
    lower = jnp.maximum(level - 1, 0)
    upper = jnp.minimum(level + 1, levels - 1)
    even = lax.rem(level, 2) == 0
    for v in range(variables):
        below = jnp.where(level > 0, coef[v, lower, 2], 0.0)
        above = jnp.where(level < levels - 1, coef[v, upper, 0], 0.0)
        mine = (coef[v, level, 1], jnp.where(even, above, below), jnp.where(even, below, above))
        for n in range(3):
            coef_out[3 * v + n : 3 * v + n + 1, :] = jnp.full((1, BLK), mine[n], jnp.float32)
    for k in range(taps):
        place = REACH - lon_offs[k]
        for half in range(2):
            rows = pl.ds(pl.multiple_of((place + half) * BLK, BLK), BLK)
            lon_out[rows, half * BLK : (half + 1) * BLK] = lon[k]
    for s in range(nblk):
        half = s % 2
        for k in range(taps):
            source = jnp.clip(s - lat_offs[k], 0, nblk - 1)
            place = REACH - lat_offs[k] + half
            rows = pl.ds(pl.multiple_of(place * BLK, BLK), BLK)
            lat_out[s // 2, rows, half * BLK : (half + 1) * BLK] = table[band[source], k]


def lat_kernel(own, chip, cross, coef, weights, out, rows_of):
    variables, _, rows, nlat = own.shape
    nblk = nlat // BLK
    zeros = jnp.zeros((variables * rows, REACH * BLK), rows_of.dtype)
    rows_of[:, : REACH * BLK] = zeros
    rows_of[:, (REACH + nblk) * BLK :] = zeros
    done = 0
    for pair in range(nblk // 2):
        ready = min(nblk, 2 * pair + SPAN - REACH)
        for t in range(done, ready):
            cols = slice(t * BLK, (t + 1) * BLK)
            for v in range(variables):
                total = coef[3 * v : 3 * v + 1, :] * own[v, 0, :, cols].astype(jnp.float32)
                total = total + coef[3 * v + 1 : 3 * v + 2, :] * chip[v, 0, :, cols].astype(
                    jnp.float32
                )
                total = total + coef[3 * v + 2 : 3 * v + 3, :] * cross[v, 0, :, cols].astype(
                    jnp.float32
                )
                rows_of[
                    v * rows : (v + 1) * rows, (REACH + t) * BLK : (REACH + t + 1) * BLK
                ] = total.astype(rows_of.dtype)
        done = ready
        total = jnp.dot(
            rows_of[:, 2 * pair * BLK : (2 * pair + SPAN) * BLK],
            weights[pair],
            preferred_element_type=jnp.float32,
        )
        out[2 * pair * BLK : 2 * (pair + 1) * BLK, :] = total.T.astype(out.dtype)


def lon_kernel(data, weights, out, rows_of, stage, sem):
    peers, lats, width = data.shape
    half = BLK // 2
    variables = width // half
    nblk = peers // 2
    rows = variables * lats
    first = lax.broadcasted_iota(jnp.int32, (lats, BLK), 1) < half
    group = 4

    def fill(t):
        spots = [p for p in (t + REACH, t + REACH + nblk, t + REACH - nblk) if 0 <= p]
        spots = [p for p in spots if p < nblk + 2 * REACH]
        for pair in range(variables // 2):
            cols = slice(pair * BLK, (pair + 1) * BLK)
            a = data[2 * t, :, cols].astype(jnp.float32)
            b = data[2 * t + 1, :, cols].astype(jnp.float32)
            even = jnp.where(first, a, pltpu.roll(b, half, 1)).astype(rows_of.dtype)
            odd = jnp.where(first, pltpu.roll(a, half, 1), b).astype(rows_of.dtype)
            v = 2 * pair
            for p in spots:
                rows_of[v * lats : (v + 1) * lats, p * BLK : (p + 1) * BLK] = even
                rows_of[(v + 1) * lats : (v + 2) * lats, p * BLK : (p + 1) * BLK] = odd

    order = [*range(nblk - REACH, nblk), *range(nblk - REACH)]
    done = 0
    for g in range(0, nblk // 2, group):
        ready = min(nblk, 2 * (g + group) + 2 * REACH)
        for t in order[done:ready]:
            fill(t)
        done = ready
        lhs = jnp.concatenate(
            [
                rows_of[:, 2 * pair * BLK : (2 * pair + SPAN) * BLK]
                for pair in range(g, g + group)
            ],
            axis=0,
        )
        total = jnp.dot(lhs, weights[...], preferred_element_type=jnp.float32)
        for n in range(group):
            for h in range(2):
                s = 2 * (g + n) + h
                stage[s] = total[n * rows : (n + 1) * rows, h * BLK : (h + 1) * BLK]
                for v in range(variables):
                    pltpu.make_async_copy(
                        stage.at[s, v * lats : (v + 1) * lats], out.at[:, v, s, 0, :], sem
                    ).start()
    pltpu.make_async_copy(stage, stage, sem).wait()


def per_device(
    increment, vert_coef, latitude_block_matrix, lat_band, lat_offsets, lon_blocks, lon_offsets
):
    variables, _, rows, nlat = increment.shape
    nblk = nlat // BLK
    npencil = lax.axis_size("pencil")
    nlev = lax.axis_size("lev")
    nlon = rows * npencil
    lats = nlat // npencil
    width = variables * rows
    nout = nlon // BLK
    vmem = pl.BlockSpec(memory_space=pltpu.VMEM)
    hbm = pl.BlockSpec(memory_space=pl.ANY)
    params = pltpu.CompilerParams(vmem_limit_bytes=32 * 2**20)

    chip_pairs = [(n, n ^ 1) for n in range(nlev)]
    cross_pairs = [p for n in range(1, nlev - 1, 2) for p in ((n, n + 1), (n + 1, n))]
    chip = lax.ppermute(increment, "lev", chip_pairs)
    cross = lax.ppermute(increment, "lev", cross_pairs)

    lat_weights, lon_weights, coef = pl.pallas_call(
        operator_kernel,
        out_shape=(
            jax.ShapeDtypeStruct((nblk // 2, SPAN * BLK, 2 * BLK), jnp.bfloat16),
            jax.ShapeDtypeStruct((SPAN * BLK, 2 * BLK), jnp.bfloat16),
            jax.ShapeDtypeStruct((16, BLK), jnp.float32),
        ),
        in_specs=[pl.BlockSpec(memory_space=pltpu.HBM)] * 6,
        out_specs=(vmem,) * 3,
        scratch_shapes=[
            pltpu.SMEM(lat_band.shape, jnp.int32),
            pltpu.SMEM(lat_offsets.shape, jnp.int32),
            pltpu.SMEM(lon_offsets.shape, jnp.int32),
            pltpu.SMEM(vert_coef.shape, jnp.float32),
            pltpu.VMEM(latitude_block_matrix.shape, jnp.bfloat16),
            pltpu.VMEM(lon_blocks.shape, jnp.bfloat16),
            pltpu.SemaphoreType.DMA((6,)),
        ],
        compiler_params=params,
        name="operators",
    )(lat_band, lat_offsets, lon_offsets, vert_coef, latitude_block_matrix, lon_blocks)

    filtered = pl.pallas_call(
        lat_kernel,
        out_shape=jax.ShapeDtypeStruct((nlat, width), jnp.bfloat16),
        in_specs=[vmem] * 5,
        out_specs=vmem,
        scratch_shapes=[pltpu.VMEM((width, nlat + 2 * REACH * BLK), jnp.bfloat16)],
        compiler_params=params,
        name="latitude",
    )(increment, chip, cross, coef, lat_weights)
    moved = lax.all_to_all(filtered, "pencil", split_axis=0, concat_axis=0, tiled=True)
    result = pl.pallas_call(
        lon_kernel,
        out_shape=jax.ShapeDtypeStruct((lats, variables, nout, 1, BLK), jnp.float32),
        in_specs=[vmem] * 2,
        out_specs=hbm,
        scratch_shapes=[
            pltpu.VMEM((lats * variables, (nout + 2 * REACH) * BLK), jnp.bfloat16),
            pltpu.VMEM((nout, lats * variables, BLK), jnp.float32),
            pltpu.SemaphoreType.DMA,
        ],
        compiler_params=params,
        name="longitude",
    )(moved.reshape(npencil, lats, width), lon_weights)
    return result.reshape(lats, variables, 1, nlon)


def solution(mesh):
    in_specs = (P(None, "lev", "pencil", None), P(), P(), P(), P(), P(), P())
    out_specs = P("pencil", None, "lev", None)
    return jax.shard_map(
        per_device, mesh=mesh, in_specs=in_specs, out_specs=out_specs, check_vma=False
    )
```

```python
import jax
import jax.numpy as jnp
from jax import lax
from jax.experimental import pallas as pl
from jax.experimental.pallas import tpu as pltpu
from jax.sharding import PartitionSpec as P

BLK = 128
REACH = 3
SPAN = 2 * REACH + 2


def operator_kernel(
    band_hbm, lat_offs_hbm, lon_offs_hbm, coef_hbm, table_hbm, lon_hbm,
    lat_out, lon_out, coef_out,
    band, lat_offs, lon_offs, coef, table, lon, sems,
):
    moves = [
        pltpu.make_async_copy(source, target, sems.at[n])
        for n, (source, target) in enumerate(
            (
                (band_hbm, band),
                (lat_offs_hbm, lat_offs),
                (lon_offs_hbm, lon_offs),
                (coef_hbm, coef),
                (table_hbm, table),
                (lon_hbm, lon),
            )
        )
    ]
    for move in moves:
        move.start()
    level = lax.axis_index("lev")
    lat_out[...] = jnp.zeros_like(lat_out)
    lon_out[...] = jnp.zeros_like(lon_out)
    for move in moves:
        move.wait()
    variables, levels, _ = coef.shape
    taps = lat_offs.shape[0]
    nblk = band.shape[0]
    lower = jnp.maximum(level - 1, 0)
    upper = jnp.minimum(level + 1, levels - 1)
    even = lax.rem(level, 2) == 0
    for v in range(variables):
        below = jnp.where(level > 0, coef[v, lower, 2], 0.0)
        above = jnp.where(level < levels - 1, coef[v, upper, 0], 0.0)
        mine = (coef[v, level, 1], jnp.where(even, above, below), jnp.where(even, below, above))
        for n in range(3):
            coef_out[3 * v + n : 3 * v + n + 1, :] = jnp.full((1, BLK), mine[n], jnp.float32)
    for k in range(taps):
        place = REACH - lon_offs[k]
        for half in range(2):
            rows = pl.ds(pl.multiple_of((place + half) * BLK, BLK), BLK)
            lon_out[rows, half * BLK : (half + 1) * BLK] = lon[k]
    for s in range(nblk):
        half = s % 2
        for k in range(taps):
            source = jnp.clip(s - lat_offs[k], 0, nblk - 1)
            place = REACH - lat_offs[k] + half
            rows = pl.ds(pl.multiple_of(place * BLK, BLK), BLK)
            lat_out[s // 2, rows, half * BLK : (half + 1) * BLK] = table[band[source], k]


def lat_kernel(own, chip, cross, coef, weights, out, rows_of):
    variables, _, rows, nlat = own.shape
    nblk = nlat // BLK
    zeros = jnp.zeros((variables * rows, REACH * BLK), rows_of.dtype)
    rows_of[:, : REACH * BLK] = zeros
    rows_of[:, (REACH + nblk) * BLK :] = zeros
    done = 0
    for pair in range(nblk // 2):
        ready = min(nblk, 2 * pair + SPAN - REACH)
        for t in range(done, ready):
            cols = slice(t * BLK, (t + 1) * BLK)
            for v in range(variables):
                total = coef[3 * v : 3 * v + 1, :] * own[v, 0, :, cols].astype(jnp.float32)
                total = total + coef[3 * v + 1 : 3 * v + 2, :] * chip[v, 0, :, cols].astype(
                    jnp.float32
                )
                total = total + coef[3 * v + 2 : 3 * v + 3, :] * cross[v, 0, :, cols].astype(
                    jnp.float32
                )
                rows_of[
                    v * rows : (v + 1) * rows, (REACH + t) * BLK : (REACH + t + 1) * BLK
                ] = total.astype(rows_of.dtype)
        done = ready
        total = jnp.dot(
            rows_of[:, 2 * pair * BLK : (2 * pair + SPAN) * BLK],
            weights[pair],
            preferred_element_type=jnp.float32,
        )
        out[2 * pair * BLK : 2 * (pair + 1) * BLK, :] = total.T.astype(out.dtype)


def lon_kernel(data, weights, out, rows_of, stage, sem):
    peers, lats, width = data.shape
    half = BLK // 2
    variables = width // half
    nblk = peers // 2
    rows = variables * lats
    first = lax.broadcasted_iota(jnp.int32, (lats, BLK), 1) < half
    group = 4

    def fill(t):
        spots = [p for p in (t + REACH, t + REACH + nblk, t + REACH - nblk) if 0 <= p]
        spots = [p for p in spots if p < nblk + 2 * REACH]
        for pair in range(variables // 2):
            cols = slice(pair * BLK, (pair + 1) * BLK)
            a = data[2 * t, :, cols].astype(jnp.float32)
            b = data[2 * t + 1, :, cols].astype(jnp.float32)
            even = jnp.where(first, a, pltpu.roll(b, half, 1)).astype(rows_of.dtype)
            odd = jnp.where(first, pltpu.roll(a, half, 1), b).astype(rows_of.dtype)
            v = 2 * pair
            for p in spots:
                rows_of[v * lats : (v + 1) * lats, p * BLK : (p + 1) * BLK] = even
                rows_of[(v + 1) * lats : (v + 2) * lats, p * BLK : (p + 1) * BLK] = odd

    order = [*range(nblk - REACH, nblk), *range(nblk - REACH)]
    done = 0
    for g in range(0, nblk // 2, group):
        ready = min(nblk, 2 * (g + group) + 2 * REACH)
        for t in order[done:ready]:
            fill(t)
        done = ready
        lhs = jnp.concatenate(
            [
                rows_of[:, 2 * pair * BLK : (2 * pair + SPAN) * BLK]
                for pair in range(g, g + group)
            ],
            axis=0,
        )
        total = jnp.dot(lhs, weights[...], preferred_element_type=jnp.float32)
        for n in range(group):
            for h in range(2):
                s = 2 * (g + n) + h
                stage[s] = total[n * rows : (n + 1) * rows, h * BLK : (h + 1) * BLK]
                for v in range(variables):
                    pltpu.make_async_copy(
                        stage.at[s, v * lats : (v + 1) * lats], out.at[:, v, s, 0, :], sem
                    ).start()
    pltpu.make_async_copy(stage, stage, sem).wait()


def per_device(
    increment, vert_coef, latitude_block_matrix, lat_band, lat_offsets, lon_blocks, lon_offsets
):
    variables, _, rows, nlat = increment.shape
    nblk = nlat // BLK
    npencil = lax.axis_size("pencil")
    nlev = lax.axis_size("lev")
    nlon = rows * npencil
    lats = nlat // npencil
    width = variables * rows
    nout = nlon // BLK
    vmem = pl.BlockSpec(memory_space=pltpu.VMEM)
    hbm = pl.BlockSpec(memory_space=pl.ANY)
    params = pltpu.CompilerParams(vmem_limit_bytes=32 * 2**20)

    chip_pairs = [(n, n ^ 1) for n in range(nlev)]
    cross_pairs = [p for n in range(1, nlev - 1, 2) for p in ((n, n + 1), (n + 1, n))]
    chip = lax.ppermute(increment, "lev", chip_pairs)
    cross = lax.ppermute(increment, "lev", cross_pairs)

    lat_weights, lon_weights, coef = pl.pallas_call(
        operator_kernel,
        out_shape=(
            jax.ShapeDtypeStruct((nblk // 2, SPAN * BLK, 2 * BLK), jnp.bfloat16),
            jax.ShapeDtypeStruct((SPAN * BLK, 2 * BLK), jnp.bfloat16),
            jax.ShapeDtypeStruct((16, BLK), jnp.float32),
        ),
        in_specs=[pl.BlockSpec(memory_space=pltpu.HBM)] * 6,
        out_specs=(vmem,) * 3,
        scratch_shapes=[
            pltpu.SMEM(lat_band.shape, jnp.int32),
            pltpu.SMEM(lat_offsets.shape, jnp.int32),
            pltpu.SMEM(lon_offsets.shape, jnp.int32),
            pltpu.SMEM(vert_coef.shape, jnp.float32),
            pltpu.VMEM(latitude_block_matrix.shape, jnp.bfloat16),
            pltpu.VMEM(lon_blocks.shape, jnp.bfloat16),
            pltpu.SemaphoreType.DMA((6,)),
        ],
        compiler_params=params,
        name="operators",
    )(
        *(
            pltpu.with_memory_space_constraint(x, pltpu.HBM)
            for x in (
                lat_band,
                lat_offsets,
                lon_offsets,
                vert_coef,
                latitude_block_matrix,
                lon_blocks,
            )
        )
    )

    filtered = pl.pallas_call(
        lat_kernel,
        out_shape=jax.ShapeDtypeStruct((nlat, width), jnp.bfloat16),
        in_specs=[vmem] * 5,
        out_specs=vmem,
        scratch_shapes=[pltpu.VMEM((width, nlat + 2 * REACH * BLK), jnp.bfloat16)],
        compiler_params=params,
        name="latitude",
    )(increment, chip, cross, coef, lat_weights)
    moved = lax.all_to_all(filtered, "pencil", split_axis=0, concat_axis=0, tiled=True)
    result = pl.pallas_call(
        lon_kernel,
        out_shape=jax.ShapeDtypeStruct((lats, variables, nout, 1, BLK), jnp.float32),
        in_specs=[vmem] * 2,
        out_specs=hbm,
        scratch_shapes=[
            pltpu.VMEM((lats * variables, (nout + 2 * REACH) * BLK), jnp.bfloat16),
            pltpu.VMEM((nout, lats * variables, BLK), jnp.float32),
            pltpu.SemaphoreType.DMA,
        ],
        compiler_params=params,
        name="longitude",
    )(moved.reshape(npencil, lats, width), lon_weights)
    return result.reshape(lats, variables, 1, nlon)


def solution(mesh):
    in_specs = (P(None, "lev", "pencil", None), P(), P(), P(), P(), P(), P())
    out_specs = P("pencil", None, "lev", None)
    return jax.shard_map(
        per_device, mesh=mesh, in_specs=in_specs, out_specs=out_specs, check_vma=False
    )
```

```python
import jax
import jax.numpy as jnp
from jax import lax
from jax.experimental import pallas as pl
from jax.experimental.pallas import tpu as pltpu
from jax.sharding import PartitionSpec as P

BLK = 128
REACH = 3
SPAN = 2 * REACH + 2


def operator_kernel(
    band_hbm, lat_offs_hbm, lon_offs_hbm, coef_hbm, table_hbm, lon_hbm,
    lat_out, lon_out, coef_out,
    band, lat_offs, lon_offs, coef, table, lon, sems,
):
    moves = [
        pltpu.make_async_copy(source, target, sems.at[n])
        for n, (source, target) in enumerate(
            (
                (band_hbm, band),
                (lat_offs_hbm, lat_offs),
                (lon_offs_hbm, lon_offs),
                (coef_hbm, coef),
                (table_hbm, table),
                (lon_hbm, lon),
            )
        )
    ]
    for move in moves:
        move.start()
    level = lax.axis_index("lev")
    lat_out[...] = jnp.zeros_like(lat_out)
    lon_out[...] = jnp.zeros_like(lon_out)
    for move in moves:
        move.wait()
    variables, levels, _ = coef.shape
    taps = lat_offs.shape[0]
    nblk = band.shape[0]
    lower = jnp.maximum(level - 1, 0)
    upper = jnp.minimum(level + 1, levels - 1)
    even = lax.rem(level, 2) == 0
    for v in range(variables):
        below = jnp.where(level > 0, coef[v, lower, 2], 0.0)
        above = jnp.where(level < levels - 1, coef[v, upper, 0], 0.0)
        mine = (coef[v, level, 1], jnp.where(even, above, below), jnp.where(even, below, above))
        for n in range(3):
            coef_out[3 * v + n : 3 * v + n + 1, :] = jnp.full((1, BLK), mine[n], jnp.float32)
    for k in range(taps):
        place = REACH - lon_offs[k]
        for half in range(2):
            rows = pl.ds(pl.multiple_of((place + half) * BLK, BLK), BLK)
            lon_out[rows, half * BLK : (half + 1) * BLK] = lon[k]
    for s in range(nblk):
        half = s % 2
        for k in range(taps):
            source = jnp.clip(s - lat_offs[k], 0, nblk - 1)
            place = REACH - lat_offs[k] + half
            rows = pl.ds(pl.multiple_of(place * BLK, BLK), BLK)
            lat_out[s // 2, rows, half * BLK : (half + 1) * BLK] = table[band[source], k]


def lat_kernel(own, chip, cross, coef, weights, out, rows_of):
    variables, _, rows, nlat = own.shape
    nblk = nlat // BLK
    zeros = jnp.zeros((variables * rows, REACH * BLK), rows_of.dtype)
    rows_of[:, : REACH * BLK] = zeros
    rows_of[:, (REACH + nblk) * BLK :] = zeros
    done = 0
    for pair in range(nblk // 2):
        ready = min(nblk, 2 * pair + SPAN - REACH)
        for t in range(done, ready):
            cols = slice(t * BLK, (t + 1) * BLK)
            for v in range(variables):
                total = coef[3 * v : 3 * v + 1, :] * own[v, 0, :, cols].astype(jnp.float32)
                total = total + coef[3 * v + 1 : 3 * v + 2, :] * chip[v, 0, :, cols].astype(
                    jnp.float32
                )
                total = total + coef[3 * v + 2 : 3 * v + 3, :] * cross[v, 0, :, cols].astype(
                    jnp.float32
                )
                rows_of[
                    v * rows : (v + 1) * rows, (REACH + t) * BLK : (REACH + t + 1) * BLK
                ] = total.astype(rows_of.dtype)
        done = ready
        total = jnp.dot(
            rows_of[:, 2 * pair * BLK : (2 * pair + SPAN) * BLK],
            weights[pair],
            preferred_element_type=jnp.float32,
        )
        out[2 * pair * BLK : 2 * (pair + 1) * BLK, :] = total.T.astype(out.dtype)


def lon_kernel(data, weights, out, rows_of, stage, sem):
    peers, lats, width = data.shape
    half = BLK // 2
    variables = width // half
    nblk = peers // 2
    rows = variables * lats
    first = lax.broadcasted_iota(jnp.int32, (lats, BLK), 1) < half

    def fill(t):
        spots = [p for p in (t + REACH, t + REACH + nblk, t + REACH - nblk) if 0 <= p]
        spots = [p for p in spots if p < nblk + 2 * REACH]
        for pair in range(variables // 2):
            cols = slice(pair * BLK, (pair + 1) * BLK)
            a = data[2 * t, :, cols].astype(jnp.float32)
            b = data[2 * t + 1, :, cols].astype(jnp.float32)
            even = jnp.where(first, a, pltpu.roll(b, half, 1)).astype(rows_of.dtype)
            odd = jnp.where(first, pltpu.roll(a, half, 1), b).astype(rows_of.dtype)
            v = 2 * pair
            for p in spots:
                rows_of[v * lats : (v + 1) * lats, p * BLK : (p + 1) * BLK] = even
                rows_of[(v + 1) * lats : (v + 2) * lats, p * BLK : (p + 1) * BLK] = odd

    order = [*range(nblk - REACH, nblk), *range(nblk - REACH)]
    done = g = 0
    for group in (1, 2, 3, 3, 3, 4):
        ready = min(nblk, 2 * (g + group) + 2 * REACH)
        for t in order[done:ready]:
            fill(t)
        done = ready
        lhs = jnp.concatenate(
            [
                rows_of[:, 2 * pair * BLK : (2 * pair + SPAN) * BLK]
                for pair in range(g, g + group)
            ],
            axis=0,
        )
        total = jnp.dot(lhs, weights[...], preferred_element_type=jnp.float32)
        for n in range(group):
            for h in range(2):
                s = 2 * (g + n) + h
                stage[s] = total[n * rows : (n + 1) * rows, h * BLK : (h + 1) * BLK]
                for v in range(variables):
                    pltpu.make_async_copy(
                        stage.at[s, v * lats : (v + 1) * lats], out.at[:, v, s, 0, :], sem
                    ).start()
        g += group
    assert 2 * g == nblk
    pltpu.make_async_copy(stage, stage, sem).wait()


def per_device(
    increment, vert_coef, latitude_block_matrix, lat_band, lat_offsets, lon_blocks, lon_offsets
):
    variables, _, rows, nlat = increment.shape
    nblk = nlat // BLK
    npencil = lax.axis_size("pencil")
    nlev = lax.axis_size("lev")
    nlon = rows * npencil
    lats = nlat // npencil
    width = variables * rows
    nout = nlon // BLK
    vmem = pl.BlockSpec(memory_space=pltpu.VMEM)
    hbm = pl.BlockSpec(memory_space=pl.ANY)
    params = pltpu.CompilerParams(vmem_limit_bytes=32 * 2**20)

    chip_pairs = [(n, n ^ 1) for n in range(nlev)]
    cross_pairs = [p for n in range(1, nlev - 1, 2) for p in ((n, n + 1), (n + 1, n))]
    chip = lax.ppermute(increment, "lev", chip_pairs)
    cross = lax.ppermute(increment, "lev", cross_pairs)

    lat_weights, lon_weights, coef = pl.pallas_call(
        operator_kernel,
        out_shape=(
            jax.ShapeDtypeStruct((nblk // 2, SPAN * BLK, 2 * BLK), jnp.bfloat16),
            jax.ShapeDtypeStruct((SPAN * BLK, 2 * BLK), jnp.bfloat16),
            jax.ShapeDtypeStruct((16, BLK), jnp.float32),
        ),
        in_specs=[pl.BlockSpec(memory_space=pltpu.HBM)] * 6,
        out_specs=(vmem,) * 3,
        scratch_shapes=[
            pltpu.SMEM(lat_band.shape, jnp.int32),
            pltpu.SMEM(lat_offsets.shape, jnp.int32),
            pltpu.SMEM(lon_offsets.shape, jnp.int32),
            pltpu.SMEM(vert_coef.shape, jnp.float32),
            pltpu.VMEM(latitude_block_matrix.shape, jnp.bfloat16),
            pltpu.VMEM(lon_blocks.shape, jnp.bfloat16),
            pltpu.SemaphoreType.DMA((6,)),
        ],
        compiler_params=params,
        name="operators",
    )(
        *(
            pltpu.with_memory_space_constraint(x, pltpu.HBM)
            for x in (
                lat_band,
                lat_offsets,
                lon_offsets,
                vert_coef,
                latitude_block_matrix,
                lon_blocks,
            )
        )
    )

    filtered = pl.pallas_call(
        lat_kernel,
        out_shape=jax.ShapeDtypeStruct((nlat, width), jnp.bfloat16),
        in_specs=[vmem] * 5,
        out_specs=vmem,
        scratch_shapes=[pltpu.VMEM((width, nlat + 2 * REACH * BLK), jnp.bfloat16)],
        compiler_params=params,
        name="latitude",
    )(increment, chip, cross, coef, lat_weights)
    moved = lax.all_to_all(filtered, "pencil", split_axis=0, concat_axis=0, tiled=True)
    result = pl.pallas_call(
        lon_kernel,
        out_shape=jax.ShapeDtypeStruct((lats, variables, nout, 1, BLK), jnp.float32),
        in_specs=[vmem] * 2,
        out_specs=hbm,
        scratch_shapes=[
            pltpu.VMEM((lats * variables, (nout + 2 * REACH) * BLK), jnp.bfloat16),
            pltpu.VMEM((nout, lats * variables, BLK), jnp.float32),
            pltpu.SemaphoreType.DMA,
        ],
        compiler_params=params,
        name="longitude",
    )(moved.reshape(npencil, lats, width), lon_weights)
    return result.reshape(lats, variables, 1, nlon)


def solution(mesh):
    in_specs = (P(None, "lev", "pencil", None), P(), P(), P(), P(), P(), P())
    out_specs = P("pencil", None, "lev", None)
    return jax.shard_map(
        per_device, mesh=mesh, in_specs=in_specs, out_specs=out_specs, check_vma=False
    )
```

```python
import jax
import jax.numpy as jnp
from jax import lax
from jax.experimental import pallas as pl
from jax.experimental.pallas import tpu as pltpu
from jax.sharding import PartitionSpec as P

BLK = 128
REACH = 3
SPAN = 2 * REACH + 2


def operator_kernel(
    band_hbm, lat_offs_hbm, lon_offs_hbm, coef_hbm, table_hbm, lon_hbm,
    lat_out, lon_out, coef_out,
    band, lat_offs, lon_offs, coef, table, lon, sems,
):
    moves = [
        pltpu.make_async_copy(source, target, sems.at[n])
        for n, (source, target) in enumerate(
            (
                (band_hbm, band),
                (lat_offs_hbm, lat_offs),
                (lon_offs_hbm, lon_offs),
                (coef_hbm, coef),
                (table_hbm, table),
                (lon_hbm, lon),
            )
        )
    ]
    for move in moves:
        move.start()
    level = lax.axis_index("lev")
    lat_out[...] = jnp.zeros_like(lat_out)
    lon_out[...] = jnp.zeros_like(lon_out)
    for move in moves:
        move.wait()
    variables, levels, _ = coef.shape
    taps = lat_offs.shape[0]
    nblk = band.shape[0]
    lower = jnp.maximum(level - 1, 0)
    upper = jnp.minimum(level + 1, levels - 1)
    even = lax.rem(level, 2) == 0
    for v in range(variables):
        below = jnp.where(level > 0, coef[v, lower, 2], 0.0)
        above = jnp.where(level < levels - 1, coef[v, upper, 0], 0.0)
        mine = (coef[v, level, 1], jnp.where(even, above, below), jnp.where(even, below, above))
        for n in range(3):
            coef_out[3 * v + n : 3 * v + n + 1, :] = jnp.full((1, BLK), mine[n], jnp.float32)
    for k in range(taps):
        place = REACH - lon_offs[k]
        for half in range(2):
            rows = pl.ds(pl.multiple_of((place + half) * BLK, BLK), BLK)
            lon_out[rows, half * BLK : (half + 1) * BLK] = lon[k]
    for s in range(nblk):
        half = s % 2
        for k in range(taps):
            source = jnp.clip(s - lat_offs[k], 0, nblk - 1)
            place = REACH - lat_offs[k] + half
            rows = pl.ds(pl.multiple_of(place * BLK, BLK), BLK)
            lat_out[s // 2, rows, half * BLK : (half + 1) * BLK] = table[band[source], k]


def lat_kernel(own, chip, cross, coef, weights, out, rows_of):
    variables, _, rows, nlat = own.shape
    nblk = nlat // BLK
    zeros = jnp.zeros((variables * rows, REACH * BLK), rows_of.dtype)
    rows_of[:, : REACH * BLK] = zeros
    rows_of[:, (REACH + nblk) * BLK :] = zeros
    done = 0
    for pair in range(nblk // 2):
        ready = nblk
        for t in range(done, ready):
            cols = slice(t * BLK, (t + 1) * BLK)
            for v in range(variables):
                total = coef[3 * v : 3 * v + 1, :] * own[v, 0, :, cols].astype(jnp.float32)
                total = total + coef[3 * v + 1 : 3 * v + 2, :] * chip[v, 0, :, cols].astype(
                    jnp.float32
                )
                total = total + coef[3 * v + 2 : 3 * v + 3, :] * cross[v, 0, :, cols].astype(
                    jnp.float32
                )
                rows_of[
                    v * rows : (v + 1) * rows, (REACH + t) * BLK : (REACH + t + 1) * BLK
                ] = total.astype(rows_of.dtype)
        done = ready
        total = jnp.dot(
            rows_of[:, 2 * pair * BLK : (2 * pair + SPAN) * BLK],
            weights[pair],
            preferred_element_type=jnp.float32,
        )
        out[2 * pair * BLK : 2 * (pair + 1) * BLK, :] = total.astype(out.dtype).T


def lon_kernel(data, weights, out, rows_of, stage, sem):
    peers, lats, width = data.shape
    half = BLK // 2
    variables = width // half
    nblk = peers // 2
    rows = variables * lats
    first = lax.broadcasted_iota(jnp.int32, (lats, BLK), 1) < half

    def fill(t):
        spots = [p for p in (t + REACH, t + REACH + nblk, t + REACH - nblk) if 0 <= p]
        spots = [p for p in spots if p < nblk + 2 * REACH]
        for pair in range(variables // 2):
            cols = slice(pair * BLK, (pair + 1) * BLK)
            a = data[2 * t, :, cols].astype(jnp.float32)
            b = data[2 * t + 1, :, cols].astype(jnp.float32)
            even = jnp.where(first, a, pltpu.roll(b, half, 1)).astype(rows_of.dtype)
            odd = jnp.where(first, pltpu.roll(a, half, 1), b).astype(rows_of.dtype)
            v = 2 * pair
            for p in spots:
                rows_of[v * lats : (v + 1) * lats, p * BLK : (p + 1) * BLK] = even
                rows_of[(v + 1) * lats : (v + 2) * lats, p * BLK : (p + 1) * BLK] = odd

    order = [*range(nblk - REACH, nblk), *range(nblk - REACH)]
    done = g = 0
    for group in (1, 2, 3, 3, 3, 4):
        ready = min(nblk, 2 * (g + group) + 2 * REACH)
        for t in order[done:ready]:
            fill(t)
        done = ready
        lhs = jnp.concatenate(
            [
                rows_of[:, 2 * pair * BLK : (2 * pair + SPAN) * BLK]
                for pair in range(g, g + group)
            ],
            axis=0,
        )
        total = jnp.dot(lhs, weights[...], preferred_element_type=jnp.float32)
        for n in range(group):
            for h in range(2):
                s = 2 * (g + n) + h
                stage[s] = total[n * rows : (n + 1) * rows, h * BLK : (h + 1) * BLK]
                for v in range(variables):
                    pltpu.make_async_copy(
                        stage.at[s, v * lats : (v + 1) * lats], out.at[:, v, s, 0, :], sem
                    ).start()
        g += group
    assert 2 * g == nblk
    pltpu.make_async_copy(stage, stage, sem).wait()


def per_device(
    increment, vert_coef, latitude_block_matrix, lat_band, lat_offsets, lon_blocks, lon_offsets
):
    variables, _, rows, nlat = increment.shape
    nblk = nlat // BLK
    npencil = lax.axis_size("pencil")
    nlev = lax.axis_size("lev")
    nlon = rows * npencil
    lats = nlat // npencil
    width = variables * rows
    nout = nlon // BLK
    vmem = pl.BlockSpec(memory_space=pltpu.VMEM)
    hbm = pl.BlockSpec(memory_space=pl.ANY)
    params = pltpu.CompilerParams(vmem_limit_bytes=32 * 2**20)

    chip_pairs = [(n, n ^ 1) for n in range(nlev)]
    cross_pairs = [p for n in range(1, nlev - 1, 2) for p in ((n, n + 1), (n + 1, n))]
    chip = lax.ppermute(increment, "lev", chip_pairs)
    cross = lax.ppermute(increment, "lev", cross_pairs)

    lat_weights, lon_weights, coef = pl.pallas_call(
        operator_kernel,
        out_shape=(
            jax.ShapeDtypeStruct((nblk // 2, SPAN * BLK, 2 * BLK), jnp.bfloat16),
            jax.ShapeDtypeStruct((SPAN * BLK, 2 * BLK), jnp.bfloat16),
            jax.ShapeDtypeStruct((16, BLK), jnp.float32),
        ),
        in_specs=[pl.BlockSpec(memory_space=pltpu.HBM)] * 6,
        out_specs=(vmem,) * 3,
        scratch_shapes=[
            pltpu.SMEM(lat_band.shape, jnp.int32),
            pltpu.SMEM(lat_offsets.shape, jnp.int32),
            pltpu.SMEM(lon_offsets.shape, jnp.int32),
            pltpu.SMEM(vert_coef.shape, jnp.float32),
            pltpu.VMEM(latitude_block_matrix.shape, jnp.bfloat16),
            pltpu.VMEM(lon_blocks.shape, jnp.bfloat16),
            pltpu.SemaphoreType.DMA((6,)),
        ],
        compiler_params=params,
        name="operators",
    )(
        *(
            pltpu.with_memory_space_constraint(x, pltpu.HBM)
            for x in (
                lat_band,
                lat_offsets,
                lon_offsets,
                vert_coef,
                latitude_block_matrix,
                lon_blocks,
            )
        )
    )

    filtered = pl.pallas_call(
        lat_kernel,
        out_shape=jax.ShapeDtypeStruct((nlat, width), jnp.bfloat16),
        in_specs=[vmem] * 5,
        out_specs=vmem,
        scratch_shapes=[pltpu.VMEM((width, nlat + 2 * REACH * BLK), jnp.bfloat16)],
        compiler_params=params,
        name="latitude",
    )(increment, chip, cross, coef, lat_weights)
    moved = lax.all_to_all(filtered, "pencil", split_axis=0, concat_axis=0, tiled=True)
    result = pl.pallas_call(
        lon_kernel,
        out_shape=jax.ShapeDtypeStruct((lats, variables, nout, 1, BLK), jnp.float32),
        in_specs=[vmem] * 2,
        out_specs=hbm,
        scratch_shapes=[
            pltpu.VMEM((lats * variables, (nout + 2 * REACH) * BLK), jnp.bfloat16),
            pltpu.VMEM((nout, lats * variables, BLK), jnp.float32),
            pltpu.SemaphoreType.DMA,
        ],
        compiler_params=params,
        name="longitude",
    )(moved.reshape(npencil, lats, width), lon_weights)
    return result.reshape(lats, variables, 1, nlon)


def solution(mesh):
    in_specs = (P(None, "lev", "pencil", None), P(), P(), P(), P(), P(), P())
    out_specs = P("pencil", None, "lev", None)
    return jax.shard_map(
        per_device, mesh=mesh, in_specs=in_specs, out_specs=out_specs, check_vma=False
    )
```
